32 devices in a mesh: groups: 2 (over y), seq: 4 (over z), dp: 4 (over x, core).
Axes of the slice: x: 2, y: 2, z: 4, core: 2. Of those that a mesh axis runs over, the one named last changes fastest.
Arguments:
- scan_input: bfloat16 [8, 512, 2048], P(('groups', 'dp'), 'seq'), parts along dimension 0, may hold values from -6 to 6
- gate_input: bfloat16 [8, 512, 2048], P(('groups', 'dp'), 'seq'), parts along dimension 0, may hold values from -6 to 6
- bmat: bfloat16 [8, 512, 128], P(('groups', 'dp'), 'seq'), parts along dimension 0, may hold values from -6 to 6
- cmat: bfloat16 [8, 512, 128], P(('groups', 'dp'), 'seq'), parts along dimension 0, may hold values from -0.5 to 0.5
- dt_raw: float32 [8, 512, 64], P(('groups', 'dp'), 'seq'), parts along dimension 0, may hold values from -4 to 4
- a_log: float32 [64], replicated
- d_skip: float32 [64], replicated, may hold values from 0.5 to 1.5
- gain: float32 [2048], replicated, may hold values from 0.1 to 1.9
- spans: int32 [8, 8, 2], P(('groups', 'dp')), parts along dimension 0, may hold values from 0 to 512, as said below
- cot: bfloat16 [8, 512, 2048], P(('groups', 'dp'), 'seq'), parts along dimension 0, may hold values from -6 to 6
Outputs:
- grad_x: bfloat16 [8, 512, 2048], P(('groups', 'dp'), 'seq'), parts along dimension 0
- grad_b: bfloat16 [8, 512, 128], P(('groups', 'dp'), 'seq'), parts along dimension 0
- grad_c: bfloat16 [8, 512, 128], P(('groups', 'dp'), 'seq'), parts along dimension 0
- grad_dt: float32 [8, 512, 64], P(('groups', 'dp'), 'seq'), parts along dimension 0
- grad_alog: float32 [128], P('groups'), parts along dimension 0
- grad_skip: float32 [128], P('groups'), parts along dimension 0
- grad_gain: float32 [4096], P('groups'), parts along dimension 0
The draws below stay inside these ranges and needn't reach their ends.
There are 2 independent parts, one for each index of `groups`. The reference program is written for one: setup_inputs(seed, part) draws one part's arguments, and reference() takes and returns one part's arrays. A program takes and returns all parts, laid end to end along the dimension named above; an argument that names none is the same for every part. Nothing has to cross between parts.
Inputs may be any that keep to these rules, and one draw needn't show every extreme that they name: For each sequence the 8 spans are in order and tile the positions: the first starts at 0, each ends (exclusive) where the next starts, the last ends at 512, none is empty.
All inputs are finite; a program needn't handle non-finite values.
Results may differ from the reference program's by a relative error of at most 0.001.
Values sent between devices are 32-bit elements; how exact they have to be, the bound alone decides.
A program may use at most 128 MiB of HBM per device.

```python
import math
import jax
import jax.numpy as jnp
from jax import lax

HEADS = 64
HEAD_DIM = 32
STATE = 128
DOCS = 8
TOK_DEV = 128
WIDTH = 2048
LENGTH = 512
BATCH = 4


def draw_a_log(key, part):
    return jax.random.uniform(key, (HEADS,), jnp.float32, math.log(1e-05), math.log(0.04))


def draw_spans(key, part):
    keys = jax.random.split(jax.random.fold_in(key, 17), BATCH)

    def single(subkey):
        picked = jax.random.permutation(subkey, LENGTH - 1)[:DOCS - 1] + 1
        cuts = jnp.sort(picked).astype(jnp.int32)
        starts = jnp.concatenate([jnp.zeros((1,), jnp.int32), cuts])
        ends = jnp.concatenate([cuts, jnp.full((1,), LENGTH, jnp.int32)])
        return jnp.stack([starts, ends], -1)
    return jax.vmap(single)(keys).astype(jnp.int32)


def steps_of(own_key, shape, cuts, low, high):
    def one(position, parts):
        heights = jax.random.uniform(jax.random.fold_in(jax.random.fold_in(own_key, 6), position), (parts,), jnp.float32, low / len(cuts), high / len(cuts))
        return jnp.repeat(jnp.exp(heights), shape[position] // parts).reshape((-1,) + (1,) * (len(shape) - position - 1))

    level = one(*cuts[0])
    for cut in cuts[1:]:
        level = level * one(*cut)
    return level


def bell_draw(rng, extent, scale, most, pieces=(), held_as=jnp.bfloat16):
    loudness = steps_of(rng, extent, pieces, -0.22, 0.18) if pieces else 1.0
    entries = jax.random.normal(rng, extent, jnp.float32) * scale * loudness
    return jnp.minimum(jnp.maximum(entries, -most), most).astype(held_as)


def setup_inputs(seed: int = 0, part: int = 0) -> dict:
    key_of = jax.random.split(jax.random.key(seed), 11)
    part_splits = jax.random.split(jax.random.fold_in(key_of[10], part), 11)
    return {
        "scan_input": bell_draw(part_splits[0], (BATCH, LENGTH, WIDTH), 1.0, 6.0, ((0, 4), (1, 4))),
        "gate_input": bell_draw(part_splits[1], (BATCH, LENGTH, WIDTH), 1.0, 6.0, ((0, 4), (1, 4))),
        "bmat": bell_draw(part_splits[2], (BATCH, LENGTH, STATE), 1.0, 6.0, ((0, 4), (1, 4))),
        "cmat": bell_draw(part_splits[3], (BATCH, LENGTH, STATE), STATE ** -0.5, 0.5, ((0, 4), (1, 4))),
        "dt_raw": bell_draw(part_splits[4], (BATCH, LENGTH, HEADS), 1.0, 4.0, ((0, 4), (1, 4)), jnp.float32),
        "a_log": draw_a_log(jax.random.fold_in(key_of[10], 71), part),
        "d_skip": jnp.clip(jax.random.uniform(key_of[6], (HEADS,), jnp.float32, 0.5, 1.5), 0.5, 1.5),
        "gain": jnp.clip(1.0 + 0.18 * jax.random.normal(key_of[7], (WIDTH,), jnp.float32), 0.1, 1.9),
        "spans": draw_spans(jax.random.fold_in(jax.random.fold_in(key_of[10], part), 71), part),
        "cot": bell_draw(part_splits[9], (BATCH, LENGTH, WIDTH), 1.0, 6.0, ((0, 4), (1, 4))),
    }


EPS = 1e-05
HI = lax.Precision.HIGHEST

def block_step(state, block):
    xb, bb, cb, lab, dtb, startb = block
    cum = jnp.cumsum(lab, 0)
    segl = jnp.cumsum(startb)
    place = jnp.arange(xb.shape[0])
    same = (place[:, None] >= place[None, :]) & (segl[:, None] == segl[None, :])
    spread = cum.T[:, :, None] - cum.T[:, None, :]
    lmat = jnp.exp(jnp.where(same[None], spread, -jnp.inf))
    gmat = jnp.dot(cb, bb.T, precision=HI)
    xdt = xb * dtb[:, :, None]
    y_intra = jnp.einsum('hij,jhp->ihp', lmat * gmat[None], xdt, precision=HI)
    win = jnp.where((segl == 0)[:, None], jnp.exp(cum), 0.0)
    y_inter = win[:, :, None] * jnp.einsum('in,hpn->ihp', cb, state, precision=HI)
    wout = jnp.exp(jnp.where((segl == segl[-1])[:, None], cum[-1][None, :] - cum, -jnp.inf))
    hloc = jnp.einsum('jhp,jn->hpn', xdt * wout[:, :, None], bb, precision=HI)
    ablk = jnp.where(segl[-1] == 0, jnp.exp(cum[-1]), 0.0)
    return (ablk[:, None, None] * state + hloc, y_intra + y_inter)

def sequence_loss(xs, bs, cs, raw, a_log, d_skip, gain, zs, flags, cotan):
    blocks_n = LENGTH // TOK_DEV
    dt = jax.nn.softplus(raw)
    la = -jnp.exp(a_log)[None, :] * dt
    blocks = (xs.reshape(blocks_n, TOK_DEV, HEADS, HEAD_DIM), bs.reshape(blocks_n, TOK_DEV, STATE), cs.reshape(blocks_n, TOK_DEV, STATE), la.reshape(blocks_n, TOK_DEV, HEADS), dt.reshape(blocks_n, TOK_DEV, HEADS), flags.reshape(blocks_n, TOK_DEV))
    start = jnp.zeros((HEADS, HEAD_DIM, STATE), xs.dtype)
    _, outs = lax.scan(block_step, start, blocks)
    y = outs.reshape(LENGTH, HEADS, HEAD_DIM) + d_skip[None, :, None] * xs.reshape(LENGTH, HEADS, HEAD_DIM)
    gated = y.reshape(LENGTH, HEADS * HEAD_DIM) * jax.nn.silu(zs)
    scale = lax.rsqrt(lax.optimization_barrier(jnp.mean(gated * gated, 1, keepdims=True)) + EPS)
    return jnp.sum(gated * scale * gain[None, :] * cotan)

def reference(scan_input, gate_input, bmat, cmat, dt_raw, a_log, d_skip, gain, spans, cot):

    def single(item):
        xb, zb, bb, cb, rb, sp, ct = item
        where_at = jnp.arange(LENGTH).astype(jnp.int32)
        flags = jnp.any(where_at[:, None] == sp[None, :, 0], 1).astype(jnp.int32)
        return jax.grad(sequence_loss, argnums=(0, 1, 2, 3, 4, 5, 6))(xb.astype(jnp.float32), bb.astype(jnp.float32), cb.astype(jnp.float32), rb, a_log, d_skip, gain, zb.astype(jnp.float32), flags, ct.astype(jnp.float32))
    grads = lax.map(single, (scan_input, gate_input, bmat, cmat, dt_raw, spans, cot))
    grad_x, grad_b, grad_c, grad_dt, grad_alog, grad_skip, grad_gain = grads
    return (grad_x.astype(jnp.bfloat16), grad_b.astype(jnp.bfloat16), grad_c.astype(jnp.bfloat16), grad_dt.astype(jnp.float32), lax.optimization_barrier(jnp.sum(grad_alog, 0)), lax.optimization_barrier(jnp.sum(grad_skip, 0)), lax.optimization_barrier(jnp.sum(grad_gain, 0)))
```

```python
import functools

import jax
import jax.numpy as jnp
from jax import lax
from jax.experimental import pallas as pl
from jax.experimental.pallas import tpu as pltpu
from jax.sharding import PartitionSpec as P

EPS = 1e-05
HI = lax.Precision.HIGHEST
F32 = jnp.float32
BF16 = jnp.bfloat16
MESH = pl.DeviceIdType.MESH
GROUP = 8


def nn(a, b):
    return lax.dot_general(a, b, (((1,), (0,)), ((), ())), preferred_element_type=F32)


def nt(a, b):
    return lax.dot_general(a, b, (((1,), (1,)), ((), ())), preferred_element_type=F32)


def tn(a, b):
    return lax.dot_general(a, b, (((0,), (0,)), ((), ())), preferred_element_type=F32)


def split(a):
    high = a.astype(BF16)
    return high, (a - high.astype(F32)).astype(BF16)


def exact_dot(a, b):
    return jnp.dot(a, b, precision=HI, preferred_element_type=F32)


def kernel(
    peers, dps, heads, hdim, rows,
    x_ref, z_ref, b_ref, c_ref, raw_ref, alog_ref, skip_ref, gain_ref, spans_ref, cot_ref,
    gx_ref, gb_ref, gc_ref, gdt_ref, red_out,
    xt, gate, dnorm, cott, gated, yns, dyt,
    hin, hend, gin, gout,
    ldt, mhigh, mlow, gmat_ref, bias_ref,
    cumr, cumc, dtr, winr, dtwoutr, skipr, ablkr, lar,
    s1, s2, sk, lastr, dgm, gcacc, gbacc, stat,
    part, seq_slots, part2, dp_slots,
    fs_send, fs_recv, bs_send, bs_recv, r1_send, r1_recv, r2_send, r2_recv,
):
    width = heads * hdim
    chunks = heads // GROUP
    span = GROUP * hdim
    tiles = span // 128
    me = lax.axis_index("seq")
    mine = lax.axis_index("dp")
    is_first = me == 0
    is_last = me == peers - 1
    right = jnp.minimum(me + 1, peers - 1)
    left = jnp.maximum(me - 1, 0)

    barrier = pltpu.get_barrier_semaphore()
    for d in range(1, peers):
        pl.semaphore_signal(
            barrier, inc=1, device_id={"seq": lax.rem(me + d, peers)}, device_id_type=MESH
        )
    for d in range(1, dps):
        pl.semaphore_signal(
            barrier, inc=1, device_id={"dp": lax.rem(mine + d, dps)}, device_id_type=MESH
        )

    def forward_copy(k):
        return pltpu.make_async_remote_copy(
            src_ref=hend.at[k], dst_ref=hin.at[k], send_sem=fs_send.at[k],
            recv_sem=fs_recv.at[k], device_id={"seq": right}, device_id_type=MESH,
        )

    def backward_copy(k):
        return pltpu.make_async_remote_copy(
            src_ref=gout.at[k], dst_ref=gin.at[k], send_sem=bs_send.at[k],
            recv_sem=bs_recv.at[k], device_id={"seq": left}, device_id_type=MESH,
        )

    raw = raw_ref[...]
    dt_c = jnp.maximum(raw, 0.0) + jnp.log1p(jnp.exp(-jnp.abs(raw)))
    rate = jnp.exp(alog_ref[...])
    la_c = -rate * dt_c
    both = jnp.concatenate([dt_c, la_c], axis=1).T
    dt = both[:heads]
    la = both[heads:]
    skip_b = jnp.broadcast_to(skip_ref[...], (rows, heads))
    skip_t = jnp.concatenate([skip_b, skip_b], axis=1).T[:heads]
    at_sub = lax.broadcasted_iota(jnp.int32, (rows, rows), 0)
    at_lane = lax.broadcasted_iota(jnp.int32, (rows, rows), 1)
    upper = jnp.where(at_sub <= at_lane, 1.0, 0.0).astype(F32)
    cum = exact_dot(la, upper)
    cum_c = jnp.concatenate([cum, cum], axis=0).T
    offset = me * rows
    seg_sub = jnp.zeros((rows, rows), jnp.int32)
    seg_lane = jnp.zeros((rows, rows), jnp.int32)
    seg_last = jnp.zeros((1, rows), jnp.int32)
    for d in range(spans_ref.shape[0]):
        start = spans_ref[d, 0] - offset
        inside = jnp.where(start >= 0, 1, 0)
        seg_sub = seg_sub + jnp.where(at_sub >= start, inside, 0)
        seg_lane = seg_lane + jnp.where(at_lane >= start, inside, 0)
        seg_last = seg_last + jnp.where(rows - 1 >= start, inside, 0)
    same = (at_sub >= at_lane) & (seg_sub == seg_lane)
    bias_ref[...] = jnp.where(same, 0.0, -jnp.inf)
    seg = seg_lane[:heads]
    cum_end = jnp.broadcast_to(cum[:, rows - 1:rows], (heads, rows))
    win = jnp.where(seg == 0, jnp.exp(cum), 0.0)
    wout = jnp.where(seg == seg_last, jnp.exp(cum_end - cum), 0.0)
    ablk = jnp.where(seg_last == 0, jnp.exp(cum_end), 0.0)
    shape3 = (chunks, GROUP, rows)
    cumr[...] = cum.reshape(shape3)
    dtr[...] = dt.reshape(shape3)
    winr[...] = win.reshape(shape3)
    dtwoutr[...] = (dt * wout).reshape(shape3)
    skipr[...] = skip_t.reshape(shape3)
    ablkr[...] = ablk.reshape(shape3)
    lar[...] = la
    for k in range(chunks):
        cumc[k, :, 0:GROUP] = cum_c[:, k * GROUP:(k + 1) * GROUP]
    bs = b_ref[...]
    cs = c_ref[...]
    gmat_ref[...] = nt(cs, bs)
    b_rows = jnp.concatenate([bs, bs], axis=0)
    b_lanes = jnp.concatenate([bs, bs], axis=1)
    c_rows = jnp.concatenate([cs, cs], axis=0)
    c_lanes = jnp.concatenate([cs, cs], axis=1)

    def per_head(ref, k):
        return jnp.broadcast_to(ref[k][:, None, :], (GROUP, hdim, rows)).reshape(span, rows)

    def over_channels(a):
        return jnp.sum(a.reshape(GROUP, hdim, rows), axis=1)

    def to_tokens_last(ref, k):
        parts = []
        for t in range(tiles):
            at = pl.multiple_of(k * span + t * 128, 128)
            parts.append(ref[:, pl.ds(at, 128)].astype(F32).T)
        return jnp.concatenate(parts, axis=0)

    pl.semaphore_wait(barrier, peers - 1 + dps - 1)

    def local_state(k, carry):
        xk = to_tokens_last(x_ref, k)
        xt[k] = xk.astype(BF16)
        high, low = split(xk * per_head(dtwoutr, k))
        hend[k] = nn(jnp.concatenate([high, low], axis=1), b_rows)

        @pl.when(is_first & (not_alone))
        def _():
            forward_copy(k).start()

        return carry

    not_alone = peers > 1
    lax.fori_loop(0, chunks, local_state, 0)

    @pl.when(is_first)
    def _():
        hin[...] = jnp.zeros(hin.shape, F32)

    @pl.when(is_last)
    def _():
        gin[...] = jnp.zeros(gin.shape, F32)

    stat[...] = jnp.zeros(stat.shape, F32)
    dgm[...] = jnp.zeros(dgm.shape, F32)
    gcacc[...] = jnp.zeros(gcacc.shape, F32)
    gbacc[...] = jnp.zeros(gbacc.shape, F32)

    def forward(k, carry):
        gmat = gmat_ref[...]
        bias = bias_ref[...]
        cc = cumc[k]
        cr = cumr[k]
        dk = dtr[k]
        for q in range(GROUP):
            decay = jnp.exp(cc[:, q:q + 1] - cr[q:q + 1, :] + bias) * dk[q:q + 1, :]
            ldt[k * GROUP + q] = decay
            high, low = split(decay * gmat)
            mhigh[k * GROUP + q] = high
            mlow[k * GROUP + q] = low
            xq = xt[k, q * hdim:(q + 1) * hdim, :]
            yns[k, q * hdim:(q + 1) * hdim, :] = nt(xq, high) + nt(xq, low)
        zk = to_tokens_last(z_ref, k)
        gatek = zk / (1.0 + jnp.exp(-zk))
        gate[k] = gatek
        cotk = to_tokens_last(cot_ref, k)
        cott[k] = cotk
        gparts = []
        for t in range(tiles):
            at = pl.multiple_of(k * span + t * 128, 128)
            gparts.append(jnp.broadcast_to(gain_ref[:, pl.ds(at, 128)], (rows, 128)).T)
        dnormk = cotk * jnp.concatenate(gparts, axis=0)
        dnorm[k] = dnormk

        @pl.when(jnp.logical_not(is_first))
        def _():
            forward_copy(k).wait_recv()
            hend[k] = per_head(ablkr, k) * hin[k] + hend[k]

        @pl.when(jnp.logical_not(is_first) & jnp.logical_not(is_last))
        def _():
            forward_copy(k).start()

        high, low = split(hin[k])
        cproj = nt(jnp.concatenate([high, low], axis=1), c_lanes)
        y = yns[k] + per_head(winr, k) * cproj
        yns[k] = y
        gk = (y + per_head(skipr, k) * xt[k].astype(F32)) * gatek
        gated[k] = gk
        stat[0:1, :] += jnp.sum(gk * gk, axis=0, keepdims=True)
        stat[1:2, :] += jnp.sum(gk * dnormk, axis=0, keepdims=True)
        return carry

    lax.fori_loop(0, chunks, forward, 0)

    scale = lax.rsqrt(stat[0:1, :] / width + EPS)
    mean = scale * stat[1:2, :] / width
    ones8 = jnp.ones((8, rows), BF16)

    def middle(k, carry):
        normed = gated[k] * scale
        dy = scale * (dnorm[k] - normed * mean) * gate[k]
        dyt[k] = dy
        high, low = split(dy * per_head(winr, k))
        gout[k] = nn(jnp.concatenate([high, low], axis=1), c_rows)

        @pl.when(is_last & (not_alone))
        def _():
            backward_copy(k).start()

        return carry

    lax.fori_loop(0, chunks, middle, 0)

    def backward(k, carry):
        dyk = dyt[k]
        dhigh, dlow = split(dyk)
        xk = xt[k]
        dx_parts = []
        total = dgm[...]
        for q in range(GROUP):
            sl = slice(q * hdim, (q + 1) * hdim)
            dh, dl, xq = dhigh[sl], dlow[sl], xk[sl]
            prod = tn(jnp.concatenate([dh, dl], axis=0), jnp.concatenate([xq, xq], axis=0))
            total = total + prod * ldt[k * GROUP + q]
            mh = mhigh[k * GROUP + q]
            ml = mlow[k * GROUP + q]
            dx_parts.append(nn(jnp.concatenate([dh, dl], axis=1), jnp.concatenate([mh, mh], axis=0)) + nn(dh, ml))
        dgm[...] = total
        dx = jnp.concatenate(dx_parts, axis=0)
        xf = xk.astype(F32)
        normed = gated[k] * scale
        ph, plo = split(cott[k] * normed)
        row = nt(ones8, ph) + nt(ones8, plo)
        for t in range(tiles):
            part[pl.ds(k * tiles + t, 1), :] = row[0:1, t * 128:(t + 1) * 128]
        s1[k] = over_channels(dyk * yns[k])
        sk[k] = over_channels(dyk * xf)
        wh, wl = split(dyk * per_head(winr, k))
        hh, hl = split(hin[k])
        gcacc[...] += tn(wh, hh) + tn(wh, hl) + tn(wl, hh)

        @pl.when(jnp.logical_not(is_last))
        def _():
            backward_copy(k).wait_recv()
            gout[k] = per_head(ablkr, k) * gin[k] + gout[k]

        @pl.when(jnp.logical_not(is_first) & jnp.logical_not(is_last))
        def _():
            backward_copy(k).start()

        gend = gin[k]
        gh, gl = split(gend)
        vproj = nt(jnp.concatenate([gh, gl], axis=1), b_lanes)
        weight = per_head(dtwoutr, k)
        dx = dx + weight * vproj
        uh, ul = split(xf * weight)
        gbacc[...] += tn(uh, gh) + tn(uh, gl) + tn(ul, gh)
        s2[k] = over_channels(dx * xf)
        lastr[k] = over_channels(gend * hend[k])
        gx = dx + per_head(skipr, k) * dyk
        for t in range(tiles):
            at = pl.multiple_of(k * span + t * 128, 128)
            gx_ref[:, pl.ds(at, 128)] = gx[t * 128:(t + 1) * 128].T.astype(BF16)
        return carry

    lax.fori_loop(0, chunks, backward, 0)

    rows_of = s2[...].reshape(heads, rows)
    dcum = s1[...].reshape(heads, rows) - rows_of
    lower = jnp.where(at_sub >= at_lane, 1.0, 0.0).astype(F32)
    dla = exact_dot(dcum, lower) + exact_dot(
        lastr[...].reshape(heads, rows), jnp.ones((rows, rows), F32)
    )
    dtall = dtr[...].reshape(heads, rows)
    sums = jnp.concatenate([sk[...].reshape(heads, rows), dla * lar[...]], axis=0)
    tail = lax.dot_general(
        jnp.ones((8, rows), F32), sums, (((1,), (1,)), ((), ())),
        precision=HI, preferred_element_type=F32,
    )
    gain_rows = width // 128
    part[gain_rows:gain_rows + 8, :] = tail

    def exchange(axis, n, position, src, slots, send, recv):
        def copy(d):
            return pltpu.make_async_remote_copy(
                src_ref=src, dst_ref=slots.at[position], send_sem=send.at[d],
                recv_sem=recv.at[d], device_id={axis: lax.rem(position + d, n)},
                device_id_type=MESH,
            )

        for d in range(1, n):
            copy(d).start()
        slots[position] = src[...]
        return copy

    def collect(n, position, slots, send, recv, src):
        for d in range(1, n):
            pltpu.make_async_remote_copy(
                src_ref=src, dst_ref=slots.at[lax.rem(position - d + n, n)],
                send_sem=send.at[d], recv_sem=recv.at[d],
                device_id={"seq": right}, device_id_type=MESH,
            ).wait_recv()
        total = slots[0]
        for d in range(1, n):
            total = total + slots[d]
        return total

    copy1 = exchange("seq", peers, me, part, seq_slots, r1_send, r1_recv)

    back = jnp.concatenate([rows_of / dtall, dla], axis=0).T
    sig = 1.0 / (1.0 + jnp.exp(-raw))
    gdt_ref[...] = (back[:, :heads] - rate * back[:, heads:]) * sig
    dg_high, dg_low = split(dgm[...])
    gc_ref[...] = (gcacc[...] + nn(dg_high, bs) + nn(dg_low, bs)).astype(BF16)
    gb_ref[...] = (gbacc[...] + tn(dg_high, cs) + tn(dg_low, cs)).astype(BF16)

    part2[...] = collect(peers, me, seq_slots, r1_send, r1_recv, part)
    copy2 = exchange("dp", dps, mine, part2, dp_slots, r2_send, r2_recv)
    red_out[...] = collect(dps, mine, dp_slots, r2_send, r2_recv, part2)
    for d in range(1, peers):
        copy1(d).wait_send()
    for d in range(1, dps):
        copy2(d).wait_send()

    @pl.when(jnp.logical_not(is_last))
    def _():
        @pl.loop(0, chunks)
        def _(k):
            forward_copy(k).wait_send()

    @pl.when(jnp.logical_not(is_first))
    def _():
        @pl.loop(0, chunks)
        def _(k):
            backward_copy(k).wait_send()


def on_device(peers, dps, scan_input, gate_input, bmat, cmat, dt_raw, a_log, d_skip, gain, spans, cot):
    rows, width = scan_input.shape[1:]
    heads = a_log.shape[0]
    hdim = width // heads
    state = bmat.shape[2]
    chunks = heads // GROUP
    span = GROUP * hdim
    red_rows = width // 128 + 8
    vmem = pl.BlockSpec(memory_space=pltpu.VMEM)
    wide = lambda dtype=F32: pltpu.VMEM((chunks, span, rows), dtype)
    states = pltpu.VMEM((chunks, span, state), F32)
    small = pltpu.VMEM((chunks, GROUP, rows), F32)
    square = pltpu.VMEM((rows, rows), F32)
    dma = pltpu.SemaphoreType.DMA
    gx, gb, gc, gdt, red = pl.pallas_call(
        functools.partial(kernel, peers, dps, heads, hdim, rows),
        out_shape=(
            jax.ShapeDtypeStruct((rows, width), BF16),
            jax.ShapeDtypeStruct((rows, state), BF16),
            jax.ShapeDtypeStruct((rows, state), BF16),
            jax.ShapeDtypeStruct((rows, heads), F32),
            jax.ShapeDtypeStruct((red_rows, 128), F32),
        ),
        in_specs=[vmem] * 8 + [pl.BlockSpec(memory_space=pltpu.SMEM), vmem],
        out_specs=(vmem,) * 5,
        scratch_shapes=[
            wide(BF16), wide(), wide(), wide(), wide(), wide(), wide(),
            states, states, states, states,
            pltpu.VMEM((heads, rows, rows), F32),
            pltpu.VMEM((heads, rows, rows), BF16),
            pltpu.VMEM((heads, rows, rows), BF16),
            square, square,
            small, pltpu.VMEM((chunks, rows, 128), F32), small, small, small, small, small,
            pltpu.VMEM((heads, rows), F32),
            small, small, small, small,
            square, pltpu.VMEM((rows, state), F32), pltpu.VMEM((rows, state), F32),
            pltpu.VMEM((8, rows), F32),
            pltpu.VMEM((red_rows, 128), F32),
            pltpu.VMEM((peers, red_rows, 128), F32),
            pltpu.VMEM((red_rows, 128), F32),
            pltpu.VMEM((dps, red_rows, 128), F32),
            dma((chunks,)), dma((chunks,)), dma((chunks,)), dma((chunks,)),
            dma((peers,)), dma((peers,)), dma((dps,)), dma((dps,)),
        ],
        compiler_params=pltpu.CompilerParams(
            collective_id=0, has_side_effects=True, vmem_limit_bytes=56 * 1024 * 1024
        ),
        name="scan_layer",
    )(
        scan_input[0], gate_input[0], bmat[0], cmat[0], dt_raw[0],
        a_log[None], d_skip[None], gain[None], spans[0], cot[0],
    )
    gain_rows = width // 128
    return (
        gx[None], gb[None], gc[None], gdt[None],
        red[gain_rows, heads:2 * heads],
        red[gain_rows, :heads],
        red[:gain_rows].reshape(width),
    )


def solution(mesh):
    return jax.shard_map(
        functools.partial(on_device, mesh.shape["seq"], mesh.shape["dp"]),
        mesh=mesh,
        in_specs=(
            P(("groups", "dp"), "seq", None),
            P(("groups", "dp"), "seq", None),
            P(("groups", "dp"), "seq", None),
            P(("groups", "dp"), "seq", None),
            P(("groups", "dp"), "seq", None),
            P(),
            P(),
            P(),
            P(("groups", "dp"), None, None),
            P(("groups", "dp"), "seq", None),
        ),
        out_specs=(
            P(("groups", "dp"), "seq", None),
            P(("groups", "dp"), "seq", None),
            P(("groups", "dp"), "seq", None),
            P(("groups", "dp"), "seq", None),
            P("groups"),
            P("groups"),
            P("groups"),
        ),
        check_vma=False,
    )
```

```python
import functools

import jax
import jax.numpy as jnp
from jax import lax
from jax.experimental import pallas as pl
from jax.experimental.pallas import tpu as pltpu
from jax.sharding import PartitionSpec as P

EPS = 1e-05
HI = lax.Precision.HIGHEST
F32 = jnp.float32
BF16 = jnp.bfloat16
MESH = pl.DeviceIdType.MESH
GROUP = 8
PIECES = 4


def nn(a, b):
    return lax.dot_general(a, b, (((1,), (0,)), ((), ())), preferred_element_type=F32)


def nt(a, b):
    return lax.dot_general(a, b, (((1,), (1,)), ((), ())), preferred_element_type=F32)


def tn(a, b):
    return lax.dot_general(a, b, (((0,), (0,)), ((), ())), preferred_element_type=F32)


def split(a):
    high = a.astype(BF16)
    return high, (a - high.astype(F32)).astype(BF16)


def exact_dot(a, b):
    return jnp.dot(a, b, precision=HI, preferred_element_type=F32)


def kernel(
    peers, dps, heads, hdim, rows,
    x_ref, z_ref, b_ref, c_ref, raw_ref, alog_ref, skip_ref, gain_ref, spans_ref, cot_ref,
    gx_ref, gb_ref, gc_ref, gdt_ref, gain_out, skip_out, alog_out,
    xt, gate, dnorm, cott, gated, yns, dyt,
    hin, hend, gin, gout,
    ldt, mhigh, mlow, gmat_ref, bias_ref,
    cumr, cumc, dtr, winr, dtwoutr, skipr, ablkr, lar,
    s1, s2, sk, lastr, dgm, gcacc, gbacc, stat,
    part, seq_slots, part2, dp_slots, part3, all_slots,
    fs_send, fs_recv, bs_send, bs_recv, r1_send, r1_recv, r2_send, r2_recv, r3_send, r3_recv,
):
    width = heads * hdim
    chunks = heads // GROUP
    span = GROUP * hdim
    tiles = span // 128
    me = lax.axis_index("seq")
    mine = lax.axis_index("dp")
    is_first = me == 0
    is_last = me == peers - 1
    right = jnp.minimum(me + 1, peers - 1)
    left = jnp.maximum(me - 1, 0)

    team = peers * dps

    def teammate(d):
        return {"seq": lax.rem(me + d // dps, peers), "dp": lax.rem(mine + d % dps, dps)}

    barrier = pltpu.get_barrier_semaphore()

    @pl.loop(1, team)
    def _(d):
        pl.semaphore_signal(barrier, inc=1, device_id=teammate(d), device_id_type=MESH)

    piece = span // PIECES

    def forward_copy(k, s):
        at = pl.ds(s * piece, piece)
        return pltpu.make_async_remote_copy(
            src_ref=hend.at[k, at], dst_ref=hin.at[k, at], send_sem=fs_send.at[k, s],
            recv_sem=fs_recv.at[k, s], device_id={"seq": right}, device_id_type=MESH,
        )

    def backward_copy(k, s):
        at = pl.ds(s * piece, piece)
        return pltpu.make_async_remote_copy(
            src_ref=gout.at[k, at], dst_ref=gin.at[k, at], send_sem=bs_send.at[k, s],
            recv_sem=bs_recv.at[k, s], device_id={"seq": left}, device_id_type=MESH,
        )

    def relay(copy, k, source, target, ends):
        keep = per_head(ablkr, k)
        for s in range(PIECES):
            at = slice(s * piece, (s + 1) * piece)
            copy(k, s).wait_recv()
            target[k, at, :] = keep[at] * source[k, at, :] + target[k, at, :]

            @pl.when(jnp.logical_not(ends))
            def _():
                copy(k, s).start()

    raw = raw_ref[...]
    dt = jnp.maximum(raw, 0.0) + jnp.log1p(jnp.exp(-jnp.abs(raw)))
    rate_b = jnp.broadcast_to(jnp.exp(alog_ref[...]), (rows, heads))
    skip_b = jnp.broadcast_to(skip_ref[...], (rows, heads))
    by_head = jnp.concatenate([skip_b, rate_b], axis=1).T
    skip_t = by_head[:heads]
    rate = by_head[heads:]
    la = -rate * dt
    at_sub = lax.broadcasted_iota(jnp.int32, (rows, rows), 0)
    at_lane = lax.broadcasted_iota(jnp.int32, (rows, rows), 1)
    upper = jnp.where(at_sub <= at_lane, 1.0, 0.0).astype(F32)
    cum = exact_dot(la, upper)
    cum_c = jnp.concatenate([cum, cum], axis=0).T
    offset = me * rows
    seg_sub = jnp.zeros((rows, rows), jnp.int32)
    seg_lane = jnp.zeros((rows, rows), jnp.int32)
    seg_last = jnp.zeros((1, rows), jnp.int32)
    for d in range(spans_ref.shape[1]):
        start = spans_ref[0, d] - offset
        inside = jnp.where(start >= 0, 1, 0)
        seg_sub = seg_sub + jnp.where(at_sub >= start, inside, 0)
        seg_lane = seg_lane + jnp.where(at_lane >= start, inside, 0)
        seg_last = seg_last + jnp.where(rows - 1 >= start, inside, 0)
    same = (at_sub >= at_lane) & (seg_sub == seg_lane)
    bias_ref[...] = jnp.where(same, 0.0, -jnp.inf)
    seg = seg_lane[:heads]
    cum_end = jnp.broadcast_to(cum[:, rows - 1:rows], (heads, rows))
    win = jnp.where(seg == 0, jnp.exp(cum), 0.0)
    wout = jnp.where(seg == seg_last, jnp.exp(cum_end - cum), 0.0)
    ablk = jnp.where(seg_last == 0, jnp.exp(cum_end), 0.0)
    shape3 = (chunks, GROUP, rows)
    cumr[...] = cum.reshape(shape3)
    dtr[...] = dt.reshape(shape3)
    winr[...] = win.reshape(shape3)
    dtwoutr[...] = (dt * wout).reshape(shape3)
    skipr[...] = skip_t.reshape(shape3)
    ablkr[...] = ablk.reshape(shape3)
    lar[...] = la
    for k in range(chunks):
        cumc[k, :, 0:GROUP] = cum_c[:, k * GROUP:(k + 1) * GROUP]
    bs = b_ref[...]
    cs = c_ref[...]
    gmat_ref[...] = nt(cs, bs)
    b_rows = jnp.concatenate([bs, bs], axis=0)
    b_lanes = jnp.concatenate([bs, bs], axis=1)
    c_rows = jnp.concatenate([cs, cs], axis=0)
    c_lanes = jnp.concatenate([cs, cs], axis=1)

    def per_head(ref, k):
        return jnp.broadcast_to(ref[k][:, None, :], (GROUP, hdim, rows)).reshape(span, rows)

    def over_channels(a):
        return jnp.sum(a.reshape(GROUP, hdim, rows), axis=1)

    def to_tokens_last(ref, k):
        parts = []
        for t in range(tiles):
            at = pl.multiple_of(k * span + t * 128, 128)
            parts.append(ref[:, pl.ds(at, 128)].astype(F32).T)
        return jnp.concatenate(parts, axis=0)

    pl.semaphore_wait(barrier, team - 1)

    def local_state(k, carry):
        xk = to_tokens_last(x_ref, k)
        xt[k] = xk.astype(BF16)
        high, low = split(xk * per_head(dtwoutr, k))
        hend[k] = nn(jnp.concatenate([high, low], axis=1), b_rows)

        @pl.when(is_first & (not_alone))
        def _():
            for s in range(PIECES):
                forward_copy(k, s).start()

        return carry

    not_alone = peers > 1
    lax.fori_loop(0, chunks, local_state, 0)

    @pl.when(is_first)
    def _():
        hin[...] = jnp.zeros(hin.shape, F32)

    @pl.when(is_last)
    def _():
        gin[...] = jnp.zeros(gin.shape, F32)

    stat[...] = jnp.zeros(stat.shape, F32)
    dgm[...] = jnp.zeros(dgm.shape, F32)
    gcacc[...] = jnp.zeros(gcacc.shape, F32)
    gbacc[...] = jnp.zeros(gbacc.shape, F32)

    def forward(k, carry):
        gmat = gmat_ref[...]
        bias = bias_ref[...]
        cc = cumc[k]
        cr = cumr[k]
        dk = dtr[k]
        for q in range(GROUP):
            decay = jnp.exp(cc[:, q:q + 1] - cr[q:q + 1, :] + bias) * dk[q:q + 1, :]
            ldt[k * GROUP + q] = decay
            high, low = split(decay * gmat)
            mhigh[k * GROUP + q] = high
            mlow[k * GROUP + q] = low
            xq = xt[k, q * hdim:(q + 1) * hdim, :]
            yns[k, q * hdim:(q + 1) * hdim, :] = nt(xq, high) + nt(xq, low)
        zk = to_tokens_last(z_ref, k)
        gatek = zk / (1.0 + jnp.exp(-zk))
        gate[k] = gatek
        cotk = to_tokens_last(cot_ref, k)
        cott[k] = cotk
        gparts = []
        for t in range(tiles):
            at = pl.multiple_of(k * span + t * 128, 128)
            gparts.append(jnp.broadcast_to(gain_ref[:, pl.ds(at, 128)], (rows, 128)).T)
        dnormk = cotk * jnp.concatenate(gparts, axis=0)
        dnorm[k] = dnormk

        @pl.when(jnp.logical_not(is_first))
        def _():
            relay(forward_copy, k, hin, hend, is_last)

        high, low = split(hin[k])
        cproj = nt(jnp.concatenate([high, low], axis=1), c_lanes)
        y = yns[k] + per_head(winr, k) * cproj
        yns[k] = y
        gk = (y + per_head(skipr, k) * xt[k].astype(F32)) * gatek
        gated[k] = gk
        stat[0:1, :] += jnp.sum(gk * gk, axis=0, keepdims=True)
        stat[1:2, :] += jnp.sum(gk * dnormk, axis=0, keepdims=True)
        return carry

    lax.fori_loop(0, chunks, forward, 0)

    scale = lax.rsqrt(stat[0:1, :] / width + EPS)
    mean = scale * stat[1:2, :] / width
    ones8 = jnp.ones((8, rows), BF16)

    def middle(k, carry):
        normed = gated[k] * scale
        dy = scale * (dnorm[k] - normed * mean) * gate[k]
        dyt[k] = dy
        high, low = split(dy * per_head(winr, k))
        gout[k] = nn(jnp.concatenate([high, low], axis=1), c_rows)

        @pl.when(is_last & (not_alone))
        def _():
            for s in range(PIECES):
                backward_copy(k, s).start()

        ph, plo = split(cott[k] * normed)
        row = nt(ones8, ph) + nt(ones8, plo)
        for t in range(tiles):
            part[pl.ds(k * tiles + t, 1), :] = row[0:1, t * 128:(t + 1) * 128]
        sk[k] = over_channels(dy * xt[k].astype(F32))
        return carry

    lax.fori_loop(0, chunks, middle, 0)

    def lane_sums(a):
        return lax.dot_general(
            jnp.ones((8, rows), F32), a, (((1,), (1,)), ((), ())),
            precision=HI, preferred_element_type=F32,
        )

    gain_rows = width // 128
    part[gain_rows:gain_rows + 8, 0:heads] = lane_sums(sk[...].reshape(heads, rows))
    part[gain_rows:gain_rows + 8, heads:128] = jnp.zeros((8, 128 - heads), F32)

    def exchange(axis, n, position, src, slots, send, recv):
        def copy(d):
            return pltpu.make_async_remote_copy(
                src_ref=src, dst_ref=slots.at[position], send_sem=send.at[d],
                recv_sem=recv.at[d], device_id={axis: lax.rem(position + d, n)},
                device_id_type=MESH,
            )

        for d in range(1, n):
            copy(d).start()
        slots[position] = src[...]
        return copy

    def collect(n, position, slots, send, recv, src):
        for d in range(1, n):
            pltpu.make_async_remote_copy(
                src_ref=src, dst_ref=slots.at[lax.rem(position - d + n, n)],
                send_sem=send.at[d], recv_sem=recv.at[d],
                device_id={"seq": right}, device_id_type=MESH,
            ).wait_recv()
        total = slots[0]
        for d in range(1, n):
            total = total + slots[d]
        return total

    copy1 = exchange("seq", peers, me, part, seq_slots, r1_send, r1_recv)

    def backward(k, carry):
        dyk = dyt[k]
        dhigh, dlow = split(dyk)
        xk = xt[k]
        dx_parts = []
        total = dgm[...]
        for q in range(GROUP):
            sl = slice(q * hdim, (q + 1) * hdim)
            dh, dl, xq = dhigh[sl], dlow[sl], xk[sl]
            prod = tn(jnp.concatenate([dh, dl], axis=0), jnp.concatenate([xq, xq], axis=0))
            total = total + prod * ldt[k * GROUP + q]
            mh = mhigh[k * GROUP + q]
            ml = mlow[k * GROUP + q]
            dx_parts.append(nn(jnp.concatenate([dh, dl], axis=1), jnp.concatenate([mh, mh], axis=0)) + nn(dh, ml))
        dgm[...] = total
        dx = jnp.concatenate(dx_parts, axis=0)
        xf = xk.astype(F32)
        s1[k] = over_channels(dyk * yns[k])
        wh, wl = split(dyk * per_head(winr, k))
        hh, hl = split(hin[k])
        gcacc[...] += tn(wh, hh) + tn(wh, hl) + tn(wl, hh)

        @pl.when(jnp.logical_not(is_last))
        def _():
            relay(backward_copy, k, gin, gout, is_first)

        gend = gin[k]
        gh, gl = split(gend)
        vproj = nt(jnp.concatenate([gh, gl], axis=1), b_lanes)
        weight = per_head(dtwoutr, k)
        dx = dx + weight * vproj
        uh, ul = split(xf * weight)
        gbacc[...] += tn(uh, gh) + tn(uh, gl) + tn(ul, gh)
        s2[k] = over_channels(dx * xf)
        lastr[k] = over_channels(gend * hend[k])
        gx = dx + per_head(skipr, k) * dyk
        for t in range(tiles):
            at = pl.multiple_of(k * span + t * 128, 128)
            gx_ref[:, pl.ds(at, 128)] = gx[t * 128:(t + 1) * 128].T.astype(BF16)
        return carry

    lax.fori_loop(0, chunks, backward, 0)

    part2[...] = collect(peers, me, seq_slots, r1_send, r1_recv, part)
    copy2 = exchange("dp", dps, mine, part2, dp_slots, r2_send, r2_recv)

    rows_of = s2[...].reshape(heads, rows)
    dcum = s1[...].reshape(heads, rows) - rows_of
    lower = jnp.where(at_sub >= at_lane, 1.0, 0.0).astype(F32)
    dla = exact_dot(dcum, lower) + exact_dot(
        lastr[...].reshape(heads, rows), jnp.ones((rows, rows), F32)
    )
    part3[:, 0:heads] = lane_sums(dla * lar[...])[0:1]
    part3[:, heads:128] = jnp.zeros((1, 128 - heads), F32)
    number = me * dps + mine

    def team_copy(d):
        return pltpu.make_async_remote_copy(
            src_ref=part3, dst_ref=all_slots.at[number], send_sem=r3_send,
            recv_sem=r3_recv, device_id=teammate(d), device_id_type=MESH,
        )

    @pl.loop(1, team)
    def _(d):
        team_copy(d).start()

    all_slots[number] = part3[...]
    gdt_ref[...] = (rows_of / dtr[...].reshape(heads, rows) - rate * dla) / (1.0 + jnp.exp(-raw))
    dg_high, dg_low = split(dgm[...])
    gc_ref[...] = (gcacc[...] + nn(dg_high, bs) + nn(dg_low, bs)).astype(BF16)
    gb_ref[...] = (gbacc[...] + tn(dg_high, cs) + tn(dg_low, cs)).astype(BF16)

    total = collect(dps, mine, dp_slots, r2_send, r2_recv, part2)
    gain_out[...] = total[0:gain_rows]
    skip_out[...] = total[gain_rows:gain_rows + 1, 0:heads]
    if team > 1:
        everyone = pltpu.make_async_copy(
            all_slots.at[pl.ds(0, team - 1)], all_slots.at[pl.ds(1, team - 1)], r3_recv
        )
        everyone.wait()
        pltpu.make_async_copy(
            all_slots.at[pl.ds(0, team - 1)], all_slots.at[pl.ds(1, team - 1)], r3_send
        ).wait()
    alog_out[...] = jnp.sum(all_slots[...], axis=0)[:, 0:heads]
    for d in range(1, peers):
        copy1(d).wait_send()
    for d in range(1, dps):
        copy2(d).wait_send()

    @pl.when(jnp.logical_not(is_last))
    def _():
        @pl.loop(0, chunks)
        def _(k):
            for s in range(PIECES):
                forward_copy(k, s).wait_send()

    @pl.when(jnp.logical_not(is_first))
    def _():
        @pl.loop(0, chunks)
        def _(k):
            for s in range(PIECES):
                backward_copy(k, s).wait_send()


def hand_over(*refs):
    n = len(refs) // 2
    for source, target in zip(refs[:n], refs[n:]):
        target[...] = source[...]


def on_device(peers, dps, scan_input, gate_input, bmat, cmat, dt_raw, a_log, d_skip, gain, spans, cot):
    rows, width = scan_input.shape[1:]
    heads = a_log.shape[0]
    hdim = width // heads
    state = bmat.shape[2]
    chunks = heads // GROUP
    span = GROUP * hdim
    red_rows = width // 128 + 8
    vmem = pl.BlockSpec(memory_space=pltpu.VMEM)
    wide = lambda dtype=F32: pltpu.VMEM((chunks, span, rows), dtype)
    states = pltpu.VMEM((chunks, span, state), F32)
    small = pltpu.VMEM((chunks, GROUP, rows), F32)
    square = pltpu.VMEM((rows, rows), F32)
    dma = pltpu.SemaphoreType.DMA
    grads = pl.pallas_call(
        functools.partial(kernel, peers, dps, heads, hdim, rows),
        out_shape=(
            jax.ShapeDtypeStruct((rows, width), BF16),
            jax.ShapeDtypeStruct((rows, state), BF16),
            jax.ShapeDtypeStruct((rows, state), BF16),
            jax.ShapeDtypeStruct((heads, rows), F32),
            jax.ShapeDtypeStruct((width // 128, 128), F32),
            jax.ShapeDtypeStruct((1, heads), F32),
            jax.ShapeDtypeStruct((1, heads), F32),
        ),
        in_specs=[vmem] * 8 + [pl.BlockSpec(memory_space=pltpu.SMEM), vmem],
        out_specs=(vmem,) * 7,
        scratch_shapes=[
            wide(BF16), wide(), wide(), wide(), wide(), wide(), wide(),
            states, states, states, states,
            pltpu.VMEM((heads, rows, rows), F32),
            pltpu.VMEM((heads, rows, rows), BF16),
            pltpu.VMEM((heads, rows, rows), BF16),
            square, square,
            small, pltpu.VMEM((chunks, rows, 128), F32), small, small, small, small, small,
            pltpu.VMEM((heads, rows), F32),
            small, small, small, small,
            square, pltpu.VMEM((rows, state), F32), pltpu.VMEM((rows, state), F32),
            pltpu.VMEM((8, rows), F32),
            pltpu.VMEM((red_rows, 128), F32),
            pltpu.VMEM((peers, red_rows, 128), F32),
            pltpu.VMEM((red_rows, 128), F32),
            pltpu.VMEM((dps, red_rows, 128), F32),
            pltpu.VMEM((1, 128), F32),
            pltpu.VMEM((peers * dps, 1, 128), F32),
            dma((chunks, PIECES)), dma((chunks, PIECES)), dma((chunks, PIECES)), dma((chunks, PIECES)),
            dma((peers,)), dma((peers,)), dma((dps,)), dma((dps,)), dma, dma,
        ],
        compiler_params=pltpu.CompilerParams(
            collective_id=0, has_side_effects=True, vmem_limit_bytes=56 * 1024 * 1024
        ),
        name="scan_layer",
    )(
        scan_input[0], gate_input[0], bmat[0], cmat[0], dt_raw[0].T,
        a_log[None], d_skip[None], gain[None], spans[0].T, cot[0],
    )
    gx, gb, gc, gdt, ggain, gskip, galog = pl.pallas_call(
        hand_over,
        out_shape=tuple(jax.ShapeDtypeStruct(g.shape, g.dtype) for g in grads),
        in_specs=[vmem] * len(grads),
        out_specs=(vmem,) * len(grads),
        name="hand_over",
    )(*grads)
    return (
        gx[None], gb[None], gc[None], gdt.T[None],
        galog.reshape(heads), gskip.reshape(heads), ggain.reshape(width),
    )


def solution(mesh):
    return jax.shard_map(
        functools.partial(on_device, mesh.shape["seq"], mesh.shape["dp"]),
        mesh=mesh,
        in_specs=(
            P(("groups", "dp"), "seq", None),
            P(("groups", "dp"), "seq", None),
            P(("groups", "dp"), "seq", None),
            P(("groups", "dp"), "seq", None),
            P(("groups", "dp"), "seq", None),
            P(),
            P(),
            P(),
            P(("groups", "dp"), None, None),
            P(("groups", "dp"), "seq", None),
        ),
        out_specs=(
            P(("groups", "dp"), "seq", None),
            P(("groups", "dp"), "seq", None),
            P(("groups", "dp"), "seq", None),
            P(("groups", "dp"), "seq", None),
            P("groups"),
            P("groups"),
            P("groups"),
        ),
        check_vma=False,
    )
```

```python
import functools

import jax
import jax.numpy as jnp
from jax import lax
from jax.experimental import pallas as pl
from jax.experimental.pallas import tpu as pltpu
from jax.sharding import PartitionSpec as P

EPS = 1e-05
HI = lax.Precision.HIGHEST
F32 = jnp.float32
BF16 = jnp.bfloat16
MESH = pl.DeviceIdType.MESH
GROUP = 8
PIECES = 4


def nn(a, b):
    return lax.dot_general(a, b, (((1,), (0,)), ((), ())), preferred_element_type=F32)


def nt(a, b):
    return lax.dot_general(a, b, (((1,), (1,)), ((), ())), preferred_element_type=F32)


def tn(a, b):
    return lax.dot_general(a, b, (((0,), (0,)), ((), ())), preferred_element_type=F32)


def split(a):
    high = a.astype(BF16)
    return high, (a - high.astype(F32)).astype(BF16)


def exact_dot(a, b):
    return jnp.dot(a, b, precision=HI, preferred_element_type=F32)


def kernel(
    peers, dps, heads, hdim, rows,
    x_ref, z_ref, b_ref, c_ref, raw_ref, alog_ref, skip_ref, gain_ref, spans_ref, cot_ref,
    gx_ref, gb_ref, gc_ref, gdt_ref, gain_out, skip_out, alog_out,
    xt, gate, dnorm, cott, gated, yns, dyt,
    hin, hend, gin, gout,
    ldt, mhigh, mlow, gmat_ref, bias_ref,
    cumr, cumc, dtr, winr, dtwoutr, skipr, ablkr, lar,
    s1, s2, sk, lastr, dgm, gcacc, gbacc, stat,
    part, seq_slots, part2, dp_slots, part3, all_slots,
    fs_send, fs_recv, bs_send, bs_recv, r1_send, r1_recv, r2_send, r2_recv, r3_send, r3_recv,
):
    width = heads * hdim
    chunks = heads // GROUP
    span = GROUP * hdim
    tiles = span // 128
    me = lax.axis_index("seq")
    mine = lax.axis_index("dp")
    is_first = me == 0
    is_last = me == peers - 1
    right = jnp.minimum(me + 1, peers - 1)
    left = jnp.maximum(me - 1, 0)

    team = peers * dps

    def teammate(d):
        return {"seq": lax.rem(me + d // dps, peers), "dp": lax.rem(mine + d % dps, dps)}

    barrier = pltpu.get_barrier_semaphore()

    @pl.when(jnp.logical_not(is_first))
    def _():
        pl.semaphore_signal(barrier, inc=1, device_id={"seq": left}, device_id_type=MESH)

    @pl.when(jnp.logical_not(is_last))
    def _():
        pl.semaphore_signal(barrier, inc=1, device_id={"seq": right}, device_id_type=MESH)

    for d in range(1, dps):
        pl.semaphore_signal(
            barrier, inc=1, device_id={"dp": lax.rem(mine + d, dps)}, device_id_type=MESH
        )

    piece = span // PIECES

    def forward_copy(k, s):
        at = pl.ds(s * piece, piece)
        return pltpu.make_async_remote_copy(
            src_ref=hend.at[k, at], dst_ref=hin.at[k, at], send_sem=fs_send.at[k, s],
            recv_sem=fs_recv.at[k, s], device_id={"seq": right}, device_id_type=MESH,
        )

    def backward_copy(k, s):
        at = pl.ds(s * piece, piece)
        return pltpu.make_async_remote_copy(
            src_ref=gout.at[k, at], dst_ref=gin.at[k, at], send_sem=bs_send.at[k, s],
            recv_sem=bs_recv.at[k, s], device_id={"seq": left}, device_id_type=MESH,
        )

    def relay(copy, k, source, target, ends):
        keep = per_head(ablkr, k)
        for s in range(PIECES):
            at = slice(s * piece, (s + 1) * piece)
            copy(k, s).wait_recv()
            target[k, at, :] = keep[at] * source[k, at, :] + target[k, at, :]

            @pl.when(jnp.logical_not(ends))
            def _():
                copy(k, s).start()

    raw = raw_ref[...]
    dt = jnp.maximum(raw, 0.0) + jnp.log1p(jnp.exp(-jnp.abs(raw)))
    rate_b = jnp.broadcast_to(jnp.exp(alog_ref[...]), (rows, heads))
    skip_b = jnp.broadcast_to(skip_ref[...], (rows, heads))
    by_head = jnp.concatenate([skip_b, rate_b], axis=1).T
    skip_t = by_head[:heads]
    rate = by_head[heads:]
    la = -rate * dt
    at_sub = lax.broadcasted_iota(jnp.int32, (rows, rows), 0)
    at_lane = lax.broadcasted_iota(jnp.int32, (rows, rows), 1)
    upper = jnp.where(at_sub <= at_lane, 1.0, 0.0).astype(F32)
    cum = exact_dot(la, upper)
    cum_c = jnp.concatenate([cum, cum], axis=0).T
    offset = me * rows
    seg_sub = jnp.zeros((rows, rows), jnp.int32)
    seg_lane = jnp.zeros((rows, rows), jnp.int32)
    seg_last = jnp.zeros((1, rows), jnp.int32)
    for d in range(spans_ref.shape[1]):
        start = spans_ref[0, d] - offset
        inside = jnp.where(start >= 0, 1, 0)
        seg_sub = seg_sub + jnp.where(at_sub >= start, inside, 0)
        seg_lane = seg_lane + jnp.where(at_lane >= start, inside, 0)
        seg_last = seg_last + jnp.where(rows - 1 >= start, inside, 0)
    same = (at_sub >= at_lane) & (seg_sub == seg_lane)
    bias_ref[...] = jnp.where(same, 0.0, -jnp.inf)
    seg = seg_lane[:heads]
    cum_end = jnp.broadcast_to(cum[:, rows - 1:rows], (heads, rows))
    win = jnp.where(seg == 0, jnp.exp(cum), 0.0)
    wout = jnp.where(seg == seg_last, jnp.exp(cum_end - cum), 0.0)
    ablk = jnp.where(seg_last == 0, jnp.exp(cum_end), 0.0)
    shape3 = (chunks, GROUP, rows)
    cumr[...] = cum.reshape(shape3)
    dtr[...] = dt.reshape(shape3)
    winr[...] = win.reshape(shape3)
    dtwoutr[...] = (dt * wout).reshape(shape3)
    skipr[...] = skip_t.reshape(shape3)
    ablkr[...] = ablk.reshape(shape3)
    lar[...] = la
    for k in range(chunks):
        cumc[k, :, 0:GROUP] = cum_c[:, k * GROUP:(k + 1) * GROUP]
    bs = b_ref[...]
    cs = c_ref[...]
    gmat_ref[...] = nt(cs, bs)
    b_rows = jnp.concatenate([bs, bs], axis=0)
    b_lanes = jnp.concatenate([bs, bs], axis=1)
    c_rows = jnp.concatenate([cs, cs], axis=0)
    c_lanes = jnp.concatenate([cs, cs], axis=1)

    def per_head(ref, k):
        return jnp.broadcast_to(ref[k][:, None, :], (GROUP, hdim, rows)).reshape(span, rows)

    def over_channels(a):
        return jnp.sum(a.reshape(GROUP, hdim, rows), axis=1)

    def to_tokens_last(ref, k):
        parts = []
        for t in range(tiles):
            at = pl.multiple_of(k * span + t * 128, 128)
            parts.append(ref[:, pl.ds(at, 128)].astype(F32).T)
        return jnp.concatenate(parts, axis=0)

    def local_state(k):
        xk = to_tokens_last(x_ref, k)
        xt[k] = xk.astype(BF16)
        high, low = split(xk * per_head(dtwoutr, k))
        hend[k] = nn(jnp.concatenate([high, low], axis=1), b_rows)

    def send_local(k):
        @pl.when(is_first & (not_alone))
        def _():
            for s in range(PIECES):
                forward_copy(k, s).start()

    not_alone = peers > 1
    local_state(0)
    pl.semaphore_wait(
        barrier, jnp.minimum(me, 1) + jnp.minimum(peers - 1 - me, 1) + dps - 1
    )
    send_local(0)

    @pl.loop(1, chunks)
    def _(k):
        local_state(k)
        send_local(k)

    @pl.when(is_first)
    def _():
        hin[...] = jnp.zeros(hin.shape, F32)

    @pl.when(is_last)
    def _():
        gin[...] = jnp.zeros(gin.shape, F32)

    stat[...] = jnp.zeros(stat.shape, F32)
    dgm[...] = jnp.zeros(dgm.shape, F32)
    gcacc[...] = jnp.zeros(gcacc.shape, F32)
    gbacc[...] = jnp.zeros(gbacc.shape, F32)

    def forward(k, carry):
        gmat = gmat_ref[...]
        bias = bias_ref[...]
        cc = cumc[k]
        cr = cumr[k]
        dk = dtr[k]
        for q in range(GROUP):
            decay = jnp.exp(cc[:, q:q + 1] - cr[q:q + 1, :] + bias) * dk[q:q + 1, :]
            ldt[k * GROUP + q] = decay
            high, low = split(decay * gmat)
            mhigh[k * GROUP + q] = high
            mlow[k * GROUP + q] = low
            xq = xt[k, q * hdim:(q + 1) * hdim, :]
            yns[k, q * hdim:(q + 1) * hdim, :] = nt(xq, high) + nt(xq, low)
        zk = to_tokens_last(z_ref, k)
        gatek = zk / (1.0 + jnp.exp(-zk))
        gate[k] = gatek
        cotk = to_tokens_last(cot_ref, k)
        cott[k] = cotk
        gparts = []
        for t in range(tiles):
            at = pl.multiple_of(k * span + t * 128, 128)
            gparts.append(jnp.broadcast_to(gain_ref[:, pl.ds(at, 128)], (rows, 128)).T)
        dnormk = cotk * jnp.concatenate(gparts, axis=0)
        dnorm[k] = dnormk

        @pl.when(jnp.logical_not(is_first))
        def _():
            relay(forward_copy, k, hin, hend, is_last)

        high, low = split(hin[k])
        cproj = nt(jnp.concatenate([high, low], axis=1), c_lanes)
        y = yns[k] + per_head(winr, k) * cproj
        yns[k] = y
        gk = (y + per_head(skipr, k) * xt[k].astype(F32)) * gatek
        gated[k] = gk
        stat[0:1, :] += jnp.sum(gk * gk, axis=0, keepdims=True)
        stat[1:2, :] += jnp.sum(gk * dnormk, axis=0, keepdims=True)
        return carry

    lax.fori_loop(0, chunks, forward, 0)

    scale = lax.rsqrt(stat[0:1, :] / width + EPS)
    mean = scale * stat[1:2, :] / width
    ones8 = jnp.ones((8, rows), BF16)

    def middle(k, carry):
        normed = gated[k] * scale
        dy = scale * (dnorm[k] - normed * mean) * gate[k]
        dyt[k] = dy
        high, low = split(dy * per_head(winr, k))
        gout[k] = nn(jnp.concatenate([high, low], axis=1), c_rows)

        @pl.when(is_last & (not_alone))
        def _():
            for s in range(PIECES):
                backward_copy(k, s).start()

        ph, plo = split(cott[k] * normed)
        row = nt(ones8, ph) + nt(ones8, plo)
        for t in range(tiles):
            part[pl.ds(k * tiles + t, 1), :] = row[0:1, t * 128:(t + 1) * 128]
        sk[k] = over_channels(dy * xt[k].astype(F32))
        return carry

    lax.fori_loop(0, chunks, middle, 0)

    def lane_sums(a):
        return lax.dot_general(
            jnp.ones((8, rows), F32), a, (((1,), (1,)), ((), ())),
            precision=HI, preferred_element_type=F32,
        )

    gain_rows = width // 128
    part[gain_rows:gain_rows + 8, 0:heads] = lane_sums(sk[...].reshape(heads, rows))
    part[gain_rows:gain_rows + 8, heads:128] = jnp.zeros((8, 128 - heads), F32)

    def exchange(axis, n, position, src, slots, send, recv):
        def copy(d):
            return pltpu.make_async_remote_copy(
                src_ref=src, dst_ref=slots.at[position], send_sem=send.at[d],
                recv_sem=recv.at[d], device_id={axis: lax.rem(position + d, n)},
                device_id_type=MESH,
            )

        for d in range(1, n):
            copy(d).start()
        slots[position] = src[...]
        return copy

    def collect(n, position, slots, send, recv, src):
        for d in range(1, n):
            pltpu.make_async_remote_copy(
                src_ref=src, dst_ref=slots.at[lax.rem(position - d + n, n)],
                send_sem=send.at[d], recv_sem=recv.at[d],
                device_id={"seq": right}, device_id_type=MESH,
            ).wait_recv()
        total = slots[0]
        for d in range(1, n):
            total = total + slots[d]
        return total

    copy1 = exchange("dp", dps, mine, part, dp_slots, r2_send, r2_recv)

    def backward(k, carry):
        dyk = dyt[k]
        dhigh, dlow = split(dyk)
        xk = xt[k]
        dx_parts = []
        total = dgm[...]
        for q in range(GROUP):
            sl = slice(q * hdim, (q + 1) * hdim)
            dh, dl, xq = dhigh[sl], dlow[sl], xk[sl]
            prod = tn(jnp.concatenate([dh, dl], axis=0), jnp.concatenate([xq, xq], axis=0))
            total = total + prod * ldt[k * GROUP + q]
            mh = mhigh[k * GROUP + q]
            ml = mlow[k * GROUP + q]
            dx_parts.append(nn(jnp.concatenate([dh, dl], axis=1), jnp.concatenate([mh, mh], axis=0)) + nn(dh, ml))
        dgm[...] = total
        dx = jnp.concatenate(dx_parts, axis=0)
        xf = xk.astype(F32)
        s1[k] = over_channels(dyk * yns[k])
        wh, wl = split(dyk * per_head(winr, k))
        hh, hl = split(hin[k])
        gcacc[...] += tn(wh, hh) + tn(wh, hl) + tn(wl, hh)

        @pl.when(jnp.logical_not(is_last))
        def _():
            relay(backward_copy, k, gin, gout, is_first)

        gend = gin[k]
        gh, gl = split(gend)
        vproj = nt(jnp.concatenate([gh, gl], axis=1), b_lanes)
        weight = per_head(dtwoutr, k)
        dx = dx + weight * vproj
        uh, ul = split(xf * weight)
        gbacc[...] += tn(uh, gh) + tn(uh, gl) + tn(ul, gh)
        s2[k] = over_channels(dx * xf)
        lastr[k] = over_channels(gend * hend[k])
        gx = dx + per_head(skipr, k) * dyk
        for t in range(tiles):
            at = pl.multiple_of(k * span + t * 128, 128)
            gx_ref[:, pl.ds(at, 128)] = gx[t * 128:(t + 1) * 128].T.astype(BF16)
        return carry

    lax.fori_loop(0, chunks - 1, backward, 0)
    part2[...] = collect(dps, mine, dp_slots, r2_send, r2_recv, part)
    copy2 = exchange("seq", peers, me, part2, seq_slots, r1_send, r1_recv)
    lax.fori_loop(chunks - 1, chunks, backward, 0)

    rows_of = s2[...].reshape(heads, rows)
    dcum = s1[...].reshape(heads, rows) - rows_of
    lower = jnp.where(at_sub >= at_lane, 1.0, 0.0).astype(F32)
    dla = exact_dot(dcum, lower) + exact_dot(
        lastr[...].reshape(heads, rows), jnp.ones((rows, rows), F32)
    )
    part3[:, 0:heads] = lane_sums(dla * lar[...])[0:1]
    part3[:, heads:128] = jnp.zeros((1, 128 - heads), F32)
    number = me * dps + mine

    def team_copy(d):
        return pltpu.make_async_remote_copy(
            src_ref=part3, dst_ref=all_slots.at[number], send_sem=r3_send,
            recv_sem=r3_recv, device_id=teammate(d), device_id_type=MESH,
        )

    @pl.loop(1, team)
    def _(d):
        team_copy(d).start()

    all_slots[number] = part3[...]
    gdt_ref[...] = (rows_of / dtr[...].reshape(heads, rows) - rate * dla) / (1.0 + jnp.exp(-raw))
    dg_high, dg_low = split(dgm[...])
    gc_ref[...] = (gcacc[...] + nn(dg_high, bs) + nn(dg_low, bs)).astype(BF16)
    gb_ref[...] = (gbacc[...] + tn(dg_high, cs) + tn(dg_low, cs)).astype(BF16)

    total = collect(peers, me, seq_slots, r1_send, r1_recv, part2)
    gain_out[...] = total[0:gain_rows]
    skip_out[...] = total[gain_rows:gain_rows + 1, 0:heads]
    if team > 1:
        everyone = pltpu.make_async_copy(
            all_slots.at[pl.ds(0, team - 1)], all_slots.at[pl.ds(1, team - 1)], r3_recv
        )
        everyone.wait()
        pltpu.make_async_copy(
            all_slots.at[pl.ds(0, team - 1)], all_slots.at[pl.ds(1, team - 1)], r3_send
        ).wait()
    alog_out[...] = jnp.sum(all_slots[...], axis=0)[:, 0:heads]
    for d in range(1, dps):
        copy1(d).wait_send()
    for d in range(1, peers):
        copy2(d).wait_send()

    @pl.when(jnp.logical_not(is_last))
    def _():
        @pl.loop(0, chunks)
        def _(k):
            for s in range(PIECES):
                forward_copy(k, s).wait_send()

    @pl.when(jnp.logical_not(is_first))
    def _():
        @pl.loop(0, chunks)
        def _(k):
            for s in range(PIECES):
                backward_copy(k, s).wait_send()


def hand_over(*refs):
    n = len(refs) // 2
    for source, target in zip(refs[:n], refs[n:]):
        target[...] = source[...]


def on_device(peers, dps, scan_input, gate_input, bmat, cmat, dt_raw, a_log, d_skip, gain, spans, cot):
    rows, width = scan_input.shape[1:]
    heads = a_log.shape[0]
    hdim = width // heads
    state = bmat.shape[2]
    chunks = heads // GROUP
    span = GROUP * hdim
    red_rows = width // 128 + 8
    vmem = pl.BlockSpec(memory_space=pltpu.VMEM)
    wide = lambda dtype=F32: pltpu.VMEM((chunks, span, rows), dtype)
    states = pltpu.VMEM((chunks, span, state), F32)
    small = pltpu.VMEM((chunks, GROUP, rows), F32)
    square = pltpu.VMEM((rows, rows), F32)
    dma = pltpu.SemaphoreType.DMA
    grads = pl.pallas_call(
        functools.partial(kernel, peers, dps, heads, hdim, rows),
        out_shape=(
            jax.ShapeDtypeStruct((rows, width), BF16),
            jax.ShapeDtypeStruct((rows, state), BF16),
            jax.ShapeDtypeStruct((rows, state), BF16),
            jax.ShapeDtypeStruct((heads, rows), F32),
            jax.ShapeDtypeStruct((width // 128, 128), F32),
            jax.ShapeDtypeStruct((1, heads), F32),
            jax.ShapeDtypeStruct((1, heads), F32),
        ),
        in_specs=[vmem] * 8 + [pl.BlockSpec(memory_space=pltpu.SMEM), vmem],
        out_specs=(vmem,) * 7,
        scratch_shapes=[
            wide(BF16), wide(), wide(), wide(), wide(), wide(), wide(),
            states, states, states, states,
            pltpu.VMEM((heads, rows, rows), F32),
            pltpu.VMEM((heads, rows, rows), BF16),
            pltpu.VMEM((heads, rows, rows), BF16),
            square, square,
            small, pltpu.VMEM((chunks, rows, 128), F32), small, small, small, small, small,
            pltpu.VMEM((heads, rows), F32),
            small, small, small, small,
            square, pltpu.VMEM((rows, state), F32), pltpu.VMEM((rows, state), F32),
            pltpu.VMEM((8, rows), F32),
            pltpu.VMEM((red_rows, 128), F32),
            pltpu.VMEM((peers, red_rows, 128), F32),
            pltpu.VMEM((red_rows, 128), F32),
            pltpu.VMEM((dps, red_rows, 128), F32),
            pltpu.VMEM((1, 128), F32),
            pltpu.VMEM((peers * dps, 1, 128), F32),
            dma((chunks, PIECES)), dma((chunks, PIECES)), dma((chunks, PIECES)), dma((chunks, PIECES)),
            dma((peers,)), dma((peers,)), dma((dps,)), dma((dps,)), dma, dma,
        ],
        compiler_params=pltpu.CompilerParams(
            collective_id=0, has_side_effects=True, vmem_limit_bytes=56 * 1024 * 1024
        ),
        name="scan_layer",
    )(
        scan_input[0], gate_input[0], bmat[0], cmat[0], dt_raw[0].T,
        a_log[None], d_skip[None], gain[None], spans[0].T, cot[0],
    )
    gx, gb, gc, gdt, ggain, gskip, galog = pl.pallas_call(
        hand_over,
        out_shape=tuple(jax.ShapeDtypeStruct(g.shape, g.dtype) for g in grads),
        in_specs=[vmem] * len(grads),
        out_specs=(vmem,) * len(grads),
        name="hand_over",
    )(*grads)
    return (
        gx[None], gb[None], gc[None], gdt.T[None],
        galog.reshape(heads), gskip.reshape(heads), ggain.reshape(width),
    )


def solution(mesh):
    return jax.shard_map(
        functools.partial(on_device, mesh.shape["seq"], mesh.shape["dp"]),
        mesh=mesh,
        in_specs=(
            P(("groups", "dp"), "seq", None),
            P(("groups", "dp"), "seq", None),
            P(("groups", "dp"), "seq", None),
            P(("groups", "dp"), "seq", None),
            P(("groups", "dp"), "seq", None),
            P(),
            P(),
            P(),
            P(("groups", "dp"), None, None),
            P(("groups", "dp"), "seq", None),
        ),
        out_specs=(
            P(("groups", "dp"), "seq", None),
            P(("groups", "dp"), "seq", None),
            P(("groups", "dp"), "seq", None),
            P(("groups", "dp"), "seq", None),
            P("groups"),
            P("groups"),
            P("groups"),
        ),
        check_vma=False,
    )
```

```python
import functools

import jax
import jax.numpy as jnp
from jax import lax
from jax.experimental import pallas as pl
from jax.experimental.pallas import tpu as pltpu
from jax.sharding import PartitionSpec as P

EPS = 1e-05
HI = lax.Precision.HIGHEST
F32 = jnp.float32
BF16 = jnp.bfloat16
MESH = pl.DeviceIdType.MESH
GROUP = 8
PIECES = 4


def nn(a, b):
    return lax.dot_general(a, b, (((1,), (0,)), ((), ())), preferred_element_type=F32)


def nt(a, b):
    return lax.dot_general(a, b, (((1,), (1,)), ((), ())), preferred_element_type=F32)


def tn(a, b):
    return lax.dot_general(a, b, (((0,), (0,)), ((), ())), preferred_element_type=F32)


def split(a):
    high = a.astype(BF16)
    return high, (a - high.astype(F32)).astype(BF16)


def exact_dot(a, b):
    return jnp.dot(a, b, precision=HI, preferred_element_type=F32)


def kernel(
    peers, dps, heads, hdim, rows,
    x_ref, z_hbm, b_ref, c_ref, raw_ref, alog_ref, skip_ref, gain_ref, spans_ref, cot_hbm,
    gx_ref, gb_ref, gc_ref, gdt_ref, gain_out, skip_out, alog_out,
    xt, gate, dnorm, cott, gated, yns, dyt,
    hin, hend, gin, gout,
    ldt, mhigh, mlow, gmat_ref, bias_ref,
    cumr, cumc, dtr, winr, dtwoutr, skipr, ablkr, lar,
    s1, s2, sk, lastr, dgm, gcacc, gbacc, stat,
    z_ref, cot_ref, in_sems, part, seq_slots, part2, dp_slots, part3, all_slots,
    fs_send, fs_recv, bs_send, bs_recv, r1_send, r1_recv, r2_send, r2_recv, r3_send, r3_recv,
):
    width = heads * hdim
    chunks = heads // GROUP
    span = GROUP * hdim
    tiles = span // 128
    me = lax.axis_index("seq")
    mine = lax.axis_index("dp")
    is_first = me == 0
    is_last = me == peers - 1
    right = jnp.minimum(me + 1, peers - 1)
    left = jnp.maximum(me - 1, 0)

    team = peers * dps
    z_copy = pltpu.make_async_copy(z_hbm, z_ref, in_sems.at[0])
    cot_copy = pltpu.make_async_copy(cot_hbm, cot_ref, in_sems.at[1])
    z_copy.start()
    cot_copy.start()

    def teammate(d):
        return {"seq": lax.rem(me + d // dps, peers), "dp": lax.rem(mine + d % dps, dps)}

    barrier = pltpu.get_barrier_semaphore()

    @pl.when(jnp.logical_not(is_first))
    def _():
        pl.semaphore_signal(barrier, inc=1, device_id={"seq": left}, device_id_type=MESH)

    @pl.when(jnp.logical_not(is_last))
    def _():
        pl.semaphore_signal(barrier, inc=1, device_id={"seq": right}, device_id_type=MESH)

    for d in range(1, dps):
        pl.semaphore_signal(
            barrier, inc=1, device_id={"dp": lax.rem(mine + d, dps)}, device_id_type=MESH
        )

    piece = span // PIECES

    def forward_copy(k, s):
        at = pl.ds(s * piece, piece)
        return pltpu.make_async_remote_copy(
            src_ref=hend.at[k, at], dst_ref=hin.at[k, at], send_sem=fs_send.at[k, s],
            recv_sem=fs_recv.at[k, s], device_id={"seq": right}, device_id_type=MESH,
        )

    def backward_copy(k, s):
        at = pl.ds(s * piece, piece)
        return pltpu.make_async_remote_copy(
            src_ref=gout.at[k, at], dst_ref=gin.at[k, at], send_sem=bs_send.at[k, s],
            recv_sem=bs_recv.at[k, s], device_id={"seq": left}, device_id_type=MESH,
        )

    def relay(copy, k, source, target, ends):
        keep = per_head(ablkr, k)
        for s in range(PIECES):
            at = slice(s * piece, (s + 1) * piece)
            copy(k, s).wait_recv()
            target[k, at, :] = keep[at] * source[k, at, :] + target[k, at, :]

            @pl.when(jnp.logical_not(ends))
            def _():
                copy(k, s).start()

    raw = raw_ref[...]
    dt = jnp.maximum(raw, 0.0) + jnp.log1p(jnp.exp(-jnp.abs(raw)))
    rate_b = jnp.broadcast_to(jnp.exp(alog_ref[...]), (rows, heads))
    skip_b = jnp.broadcast_to(skip_ref[...], (rows, heads))
    by_head = jnp.concatenate([skip_b, rate_b], axis=1).T
    skip_t = by_head[:heads]
    rate = by_head[heads:]
    la = -rate * dt
    at_sub = lax.broadcasted_iota(jnp.int32, (rows, rows), 0)
    at_lane = lax.broadcasted_iota(jnp.int32, (rows, rows), 1)
    upper = jnp.where(at_sub <= at_lane, 1.0, 0.0).astype(F32)
    cum = exact_dot(la, upper)
    cum_c = jnp.concatenate([cum, cum], axis=0).T
    offset = me * rows
    seg_sub = jnp.zeros((rows, rows), jnp.int32)
    seg_lane = jnp.zeros((rows, rows), jnp.int32)
    seg_last = jnp.zeros((1, rows), jnp.int32)
    for d in range(spans_ref.shape[1]):
        start = spans_ref[0, d] - offset
        inside = jnp.where(start >= 0, 1, 0)
        seg_sub = seg_sub + jnp.where(at_sub >= start, inside, 0)
        seg_lane = seg_lane + jnp.where(at_lane >= start, inside, 0)
        seg_last = seg_last + jnp.where(rows - 1 >= start, inside, 0)
    same = (at_sub >= at_lane) & (seg_sub == seg_lane)
    bias_ref[...] = jnp.where(same, 0.0, -jnp.inf)
    seg = seg_lane[:heads]
    cum_end = jnp.broadcast_to(cum[:, rows - 1:rows], (heads, rows))
    win = jnp.where(seg == 0, jnp.exp(cum), 0.0)
    wout = jnp.where(seg == seg_last, jnp.exp(cum_end - cum), 0.0)
    ablk = jnp.where(seg_last == 0, jnp.exp(cum_end), 0.0)
    shape3 = (chunks, GROUP, rows)
    cumr[...] = cum.reshape(shape3)
    dtr[...] = dt.reshape(shape3)
    winr[...] = win.reshape(shape3)
    dtwoutr[...] = (dt * wout).reshape(shape3)
    skipr[...] = skip_t.reshape(shape3)
    ablkr[...] = ablk.reshape(shape3)
    lar[...] = la
    for k in range(chunks):
        cumc[k, :, 0:GROUP] = cum_c[:, k * GROUP:(k + 1) * GROUP]
    bs = b_ref[...]
    cs = c_ref[...]
    gmat_ref[...] = nt(cs, bs)
    b_rows = jnp.concatenate([bs, bs], axis=0)
    b_lanes = jnp.concatenate([bs, bs], axis=1)
    c_rows = jnp.concatenate([cs, cs], axis=0)
    c_lanes = jnp.concatenate([cs, cs], axis=1)

    def per_head(ref, k):
        return jnp.broadcast_to(ref[k][:, None, :], (GROUP, hdim, rows)).reshape(span, rows)

    def over_channels(a):
        return jnp.sum(a.reshape(GROUP, hdim, rows), axis=1)

    def to_tokens_last(ref, k):
        parts = []
        for t in range(tiles):
            at = pl.multiple_of(k * span + t * 128, 128)
            parts.append(ref[:, pl.ds(at, 128)].astype(F32).T)
        return jnp.concatenate(parts, axis=0)

    def local_state(k):
        xk = to_tokens_last(x_ref, k)
        xt[k] = xk.astype(BF16)
        high, low = split(xk * per_head(dtwoutr, k))
        hend[k] = nn(jnp.concatenate([high, low], axis=1), b_rows)

    def send_local(k):
        @pl.when(is_first & (not_alone))
        def _():
            for s in range(PIECES):
                forward_copy(k, s).start()

    not_alone = peers > 1
    local_state(0)
    pl.semaphore_wait(
        barrier, jnp.minimum(me, 1) + jnp.minimum(peers - 1 - me, 1) + dps - 1
    )
    send_local(0)

    @pl.loop(1, chunks)
    def _(k):
        local_state(k)
        send_local(k)

    @pl.when(is_first)
    def _():
        hin[...] = jnp.zeros(hin.shape, F32)

    @pl.when(is_last)
    def _():
        gin[...] = jnp.zeros(gin.shape, F32)

    stat[...] = jnp.zeros(stat.shape, F32)
    dgm[...] = jnp.zeros(dgm.shape, F32)
    gcacc[...] = jnp.zeros(gcacc.shape, F32)
    gbacc[...] = jnp.zeros(gbacc.shape, F32)

    def forward(k, carry):
        gmat = gmat_ref[...]
        bias = bias_ref[...]
        cc = cumc[k]
        cr = cumr[k]
        dk = dtr[k]
        for q in range(GROUP):
            decay = jnp.exp(cc[:, q:q + 1] - cr[q:q + 1, :] + bias) * dk[q:q + 1, :]
            ldt[k * GROUP + q] = decay
            high, low = split(decay * gmat)
            mhigh[k * GROUP + q] = high
            mlow[k * GROUP + q] = low
            xq = xt[k, q * hdim:(q + 1) * hdim, :]
            yns[k, q * hdim:(q + 1) * hdim, :] = nt(xq, high) + nt(xq, low)
        zk = to_tokens_last(z_ref, k)
        gatek = zk / (1.0 + jnp.exp(-zk))
        gate[k] = gatek
        cotk = to_tokens_last(cot_ref, k)
        cott[k] = cotk
        gparts = []
        for t in range(tiles):
            at = pl.multiple_of(k * span + t * 128, 128)
            gparts.append(jnp.broadcast_to(gain_ref[:, pl.ds(at, 128)], (rows, 128)).T)
        dnormk = cotk * jnp.concatenate(gparts, axis=0)
        dnorm[k] = dnormk

        @pl.when(jnp.logical_not(is_first))
        def _():
            relay(forward_copy, k, hin, hend, is_last)

        high, low = split(hin[k])
        cproj = nt(jnp.concatenate([high, low], axis=1), c_lanes)
        y = yns[k] + per_head(winr, k) * cproj
        yns[k] = y
        gk = (y + per_head(skipr, k) * xt[k].astype(F32)) * gatek
        gated[k] = gk
        stat[0:1, :] += jnp.sum(gk * gk, axis=0, keepdims=True)
        stat[1:2, :] += jnp.sum(gk * dnormk, axis=0, keepdims=True)
        return carry

    z_copy.wait()
    cot_copy.wait()
    lax.fori_loop(0, chunks, forward, 0)

    scale = lax.rsqrt(stat[0:1, :] / width + EPS)
    mean = scale * stat[1:2, :] / width
    ones8 = jnp.ones((8, rows), BF16)

    def middle(k, carry):
        normed = gated[k] * scale
        dy = scale * (dnorm[k] - normed * mean) * gate[k]
        dyt[k] = dy
        high, low = split(dy * per_head(winr, k))
        gout[k] = nn(jnp.concatenate([high, low], axis=1), c_rows)

        @pl.when(is_last & (not_alone))
        def _():
            for s in range(PIECES):
                backward_copy(k, s).start()

        ph, plo = split(cott[k] * normed)
        row = nt(ones8, ph) + nt(ones8, plo)
        for t in range(tiles):
            part[pl.ds(k * tiles + t, 1), :] = row[0:1, t * 128:(t + 1) * 128]
        sk[k] = over_channels(dy * xt[k].astype(F32))
        return carry

    lax.fori_loop(0, chunks, middle, 0)

    def lane_sums(a):
        return lax.dot_general(
            jnp.ones((8, rows), F32), a, (((1,), (1,)), ((), ())),
            precision=HI, preferred_element_type=F32,
        )

    gain_rows = width // 128
    part[gain_rows:gain_rows + 8, 0:heads] = lane_sums(sk[...].reshape(heads, rows))
    part[gain_rows:gain_rows + 8, heads:128] = jnp.zeros((8, 128 - heads), F32)

    def exchange(axis, n, position, src, slots, send, recv):
        def copy(d):
            return pltpu.make_async_remote_copy(
                src_ref=src, dst_ref=slots.at[position], send_sem=send.at[d],
                recv_sem=recv.at[d], device_id={axis: lax.rem(position + d, n)},
                device_id_type=MESH,
            )

        for d in range(1, n):
            copy(d).start()
        slots[position] = src[...]
        return copy

    def collect(n, position, slots, send, recv, src):
        for d in range(1, n):
            pltpu.make_async_remote_copy(
                src_ref=src, dst_ref=slots.at[lax.rem(position - d + n, n)],
                send_sem=send.at[d], recv_sem=recv.at[d],
                device_id={"seq": right}, device_id_type=MESH,
            ).wait_recv()
        total = slots[0]
        for d in range(1, n):
            total = total + slots[d]
        return total

    copy1 = exchange("dp", dps, mine, part, dp_slots, r2_send, r2_recv)

    def backward(k, carry):
        dyk = dyt[k]
        dhigh, dlow = split(dyk)
        xk = xt[k]
        dx_parts = []
        total = dgm[...]
        for q in range(GROUP):
            sl = slice(q * hdim, (q + 1) * hdim)
            dh, dl, xq = dhigh[sl], dlow[sl], xk[sl]
            prod = tn(jnp.concatenate([dh, dl], axis=0), jnp.concatenate([xq, xq], axis=0))
            total = total + prod * ldt[k * GROUP + q]
            mh = mhigh[k * GROUP + q]
            ml = mlow[k * GROUP + q]
            dx_parts.append(nn(jnp.concatenate([dh, dl], axis=1), jnp.concatenate([mh, mh], axis=0)) + nn(dh, ml))
        dgm[...] = total
        dx = jnp.concatenate(dx_parts, axis=0)
        xf = xk.astype(F32)
        s1[k] = over_channels(dyk * yns[k])
        wh, wl = split(dyk * per_head(winr, k))
        hh, hl = split(hin[k])
        gcacc[...] += tn(wh, hh) + tn(wh, hl) + tn(wl, hh)

        @pl.when(jnp.logical_not(is_last))
        def _():
            relay(backward_copy, k, gin, gout, is_first)

        gend = gin[k]
        gh, gl = split(gend)
        vproj = nt(jnp.concatenate([gh, gl], axis=1), b_lanes)
        weight = per_head(dtwoutr, k)
        dx = dx + weight * vproj
        uh, ul = split(xf * weight)
        gbacc[...] += tn(uh, gh) + tn(uh, gl) + tn(ul, gh)
        s2[k] = over_channels(dx * xf)
        lastr[k] = over_channels(gend * hend[k])
        gx = dx + per_head(skipr, k) * dyk
        for t in range(tiles):
            at = pl.multiple_of(k * span + t * 128, 128)
            gx_ref[:, pl.ds(at, 128)] = gx[t * 128:(t + 1) * 128].T.astype(BF16)
        return carry

    lax.fori_loop(0, chunks - 1, backward, 0)
    part2[...] = collect(dps, mine, dp_slots, r2_send, r2_recv, part)
    copy2 = exchange("seq", peers, me, part2, seq_slots, r1_send, r1_recv)
    lax.fori_loop(chunks - 1, chunks, backward, 0)

    rows_of = s2[...].reshape(heads, rows)
    dcum = s1[...].reshape(heads, rows) - rows_of
    lower = jnp.where(at_sub >= at_lane, 1.0, 0.0).astype(F32)
    dla = exact_dot(dcum, lower) + exact_dot(
        lastr[...].reshape(heads, rows), jnp.ones((rows, rows), F32)
    )
    part3[:, 0:heads] = lane_sums(dla * lar[...])[0:1]
    part3[:, heads:128] = jnp.zeros((1, 128 - heads), F32)
    number = me * dps + mine

    def team_copy(d):
        return pltpu.make_async_remote_copy(
            src_ref=part3, dst_ref=all_slots.at[number], send_sem=r3_send,
            recv_sem=r3_recv, device_id=teammate(d), device_id_type=MESH,
        )

    @pl.loop(1, team)
    def _(d):
        team_copy(d).start()

    all_slots[number] = part3[...]
    gdt_ref[...] = (rows_of / dtr[...].reshape(heads, rows) - rate * dla) / (1.0 + jnp.exp(-raw))
    dg_high, dg_low = split(dgm[...])
    gc_ref[...] = (gcacc[...] + nn(dg_high, bs) + nn(dg_low, bs)).astype(BF16)
    gb_ref[...] = (gbacc[...] + tn(dg_high, cs) + tn(dg_low, cs)).astype(BF16)

    total = collect(peers, me, seq_slots, r1_send, r1_recv, part2)
    gain_out[...] = total[0:gain_rows]
    skip_out[...] = total[gain_rows:gain_rows + 1, 0:heads]
    if team > 1:
        everyone = pltpu.make_async_copy(
            all_slots.at[pl.ds(0, team - 1)], all_slots.at[pl.ds(1, team - 1)], r3_recv
        )
        everyone.wait()
        pltpu.make_async_copy(
            all_slots.at[pl.ds(0, team - 1)], all_slots.at[pl.ds(1, team - 1)], r3_send
        ).wait()
    alog_out[...] = jnp.sum(all_slots[...], axis=0)[:, 0:heads]
    for d in range(1, dps):
        copy1(d).wait_send()
    for d in range(1, peers):
        copy2(d).wait_send()

    @pl.when(jnp.logical_not(is_last))
    def _():
        @pl.loop(0, chunks)
        def _(k):
            for s in range(PIECES):
                forward_copy(k, s).wait_send()

    @pl.when(jnp.logical_not(is_first))
    def _():
        @pl.loop(0, chunks)
        def _(k):
            for s in range(PIECES):
                backward_copy(k, s).wait_send()


def hand_over(*refs):
    n = len(refs) // 2
    for source, target in zip(refs[:n], refs[n:]):
        target[...] = source[...]


def on_device(peers, dps, scan_input, gate_input, bmat, cmat, dt_raw, a_log, d_skip, gain, spans, cot):
    rows, width = scan_input.shape[1:]
    heads = a_log.shape[0]
    hdim = width // heads
    state = bmat.shape[2]
    chunks = heads // GROUP
    span = GROUP * hdim
    red_rows = width // 128 + 8
    vmem = pl.BlockSpec(memory_space=pltpu.VMEM)
    anywhere = pl.BlockSpec(memory_space=pl.ANY)
    wide = lambda dtype=F32: pltpu.VMEM((chunks, span, rows), dtype)
    states = pltpu.VMEM((chunks, span, state), F32)
    small = pltpu.VMEM((chunks, GROUP, rows), F32)
    square = pltpu.VMEM((rows, rows), F32)
    dma = pltpu.SemaphoreType.DMA
    grads = pl.pallas_call(
        functools.partial(kernel, peers, dps, heads, hdim, rows),
        out_shape=(
            jax.ShapeDtypeStruct((rows, width), BF16),
            jax.ShapeDtypeStruct((rows, state), BF16),
            jax.ShapeDtypeStruct((rows, state), BF16),
            jax.ShapeDtypeStruct((heads, rows), F32),
            jax.ShapeDtypeStruct((width // 128, 128), F32),
            jax.ShapeDtypeStruct((1, heads), F32),
            jax.ShapeDtypeStruct((1, heads), F32),
        ),
        in_specs=[vmem, anywhere] + [vmem] * 6 + [pl.BlockSpec(memory_space=pltpu.SMEM), anywhere],
        out_specs=(vmem,) * 7,
        scratch_shapes=[
            wide(BF16), wide(), wide(), wide(), wide(), wide(), wide(),
            states, states, states, states,
            pltpu.VMEM((heads, rows, rows), F32),
            pltpu.VMEM((heads, rows, rows), BF16),
            pltpu.VMEM((heads, rows, rows), BF16),
            square, square,
            small, pltpu.VMEM((chunks, rows, 128), F32), small, small, small, small, small,
            pltpu.VMEM((heads, rows), F32),
            small, small, small, small,
            square, pltpu.VMEM((rows, state), F32), pltpu.VMEM((rows, state), F32),
            pltpu.VMEM((8, rows), F32),
            pltpu.VMEM((rows, width), BF16), pltpu.VMEM((rows, width), BF16), pltpu.SemaphoreType.DMA((2,)),
            pltpu.VMEM((red_rows, 128), F32),
            pltpu.VMEM((peers, red_rows, 128), F32),
            pltpu.VMEM((red_rows, 128), F32),
            pltpu.VMEM((dps, red_rows, 128), F32),
            pltpu.VMEM((1, 128), F32),
            pltpu.VMEM((peers * dps, 1, 128), F32),
            dma((chunks, PIECES)), dma((chunks, PIECES)), dma((chunks, PIECES)), dma((chunks, PIECES)),
            dma((peers,)), dma((peers,)), dma((dps,)), dma((dps,)), dma, dma,
        ],
        compiler_params=pltpu.CompilerParams(
            collective_id=0, has_side_effects=True, vmem_limit_bytes=56 * 1024 * 1024
        ),
        name="scan_layer",
    )(
        scan_input[0], gate_input[0], bmat[0], cmat[0], dt_raw[0].T,
        a_log[None], d_skip[None], gain[None], spans[0].T, cot[0],
    )
    gx, gb, gc, gdt, ggain, gskip, galog = pl.pallas_call(
        hand_over,
        out_shape=tuple(jax.ShapeDtypeStruct(g.shape, g.dtype) for g in grads),
        in_specs=[vmem] * len(grads),
        out_specs=(vmem,) * len(grads),
        name="hand_over",
    )(*grads)
    return (
        gx[None], gb[None], gc[None], gdt.T[None],
        galog.reshape(heads), gskip.reshape(heads), ggain.reshape(width),
    )


def solution(mesh):
    return jax.shard_map(
        functools.partial(on_device, mesh.shape["seq"], mesh.shape["dp"]),
        mesh=mesh,
        in_specs=(
            P(("groups", "dp"), "seq", None),
            P(("groups", "dp"), "seq", None),
            P(("groups", "dp"), "seq", None),
            P(("groups", "dp"), "seq", None),
            P(("groups", "dp"), "seq", None),
            P(),
            P(),
            P(),
            P(("groups", "dp"), None, None),
            P(("groups", "dp"), "seq", None),
        ),
        out_specs=(
            P(("groups", "dp"), "seq", None),
            P(("groups", "dp"), "seq", None),
            P(("groups", "dp"), "seq", None),
            P(("groups", "dp"), "seq", None),
            P("groups"),
            P("groups"),
            P("groups"),
        ),
        check_vma=False,
    )
```
